256 devices in a mesh: area: 32 (over z, x), unit: 8 (over y, core).
Axes of the slice: x: 4, y: 4, z: 8, core: 2. Of those that a mesh axis runs over, the one named last changes fastest.
Arguments:
- initial_rates: float32 [32, 4096, 128], P('area', 'unit'), may hold values from -0.9 to 0.9
- prior_rates: bfloat16 [32, 4096, 128], P('area', 'unit'), may hold values from -0.8984375 to 0.8984375
- local_weight: bfloat16 [32, 4096, 4096], P('area', 'unit'), may hold values from -0.125 to 0.125
- long_weight: bfloat16 [32, 4096, 2048], P('area', 'unit'), may hold values from -0.1875 to 0.1875
- input_weight: bfloat16 [32, 4096, 16], P('area', 'unit'), may hold values from -1.5 to 1.5
- unit_bias: float32 [32, 4096], P('area', 'unit'), may hold values from -2.5 to 2.5
- leak_rate: float32 [32, 4096], P('area', 'unit'), may hold values from 0.2 to 1
- stimulus: bfloat16 [6, 16, 128], replicated, may hold values from -4 to 4
- link_source: int32 [32, 16], replicated, may hold values from 0 to 31, as said below
- link_block: int32 [32, 16], replicated, may hold values from 0 to 31
- link_delay: int32 [32, 16], replicated, may hold values from 0 to 1
Outputs:
- final_rates: float32 [32, 4096, 128], P('area', 'unit')
- final_current: float32 [32, 4096, 128], P('area', 'unit')
The draws below stay inside these ranges and needn't reach their ends.
Inputs may be any that keep to these rules, and one draw needn't show every extreme that they name: `link_source`: each area's 16 entries name every source area at most 1 times, and some source area exactly 1 times.
All inputs are finite; a program needn't handle non-finite values.
Results may differ from the reference program's by a relative error of at most 0.004.
Values may be sent and summed in bfloat16 or wider, within the bound.
No kernel may reach another device: no remote copies, remote signals or barrier semaphores. Data moves between devices by JAX's collectives and lax.ppermute only.
A program may use at most 64 MiB of HBM per device.

```python
import math
import jax
import jax.numpy as jnp
from jax import lax

UNITS = 4096
BLOCK = 128
SLOTS = 16
STIM = 16
WINDOWS = 3
TRIALS = 128
AREAS = 32
INPUTS = 2048
STEPS = 6


def draw_link_source(key, part):
    per_pair = max(1, (SLOTS + AREAS - 1) // AREAS)
    candidates = AREAS * per_pair
    first_key, second_key = jax.random.split(jax.random.fold_in(key, 11))
    favour = jax.random.randint(first_key, (AREAS,), 0, 4) * 400
    jitter = jax.random.randint(second_key, (AREAS, candidates), 0, 1000)
    area_of = jnp.arange(candidates, dtype=jnp.int32) // per_pair
    scores = (jitter + favour[area_of][None, :]) * candidates + jnp.arange(candidates, dtype=jnp.int32)[None, :]
    ignored, picked = lax.top_k(scores, SLOTS)
    return (picked // per_pair).astype(jnp.int32)


def with_ends(array, own_key, smallest, top_value):
    longest = array.shape.index(max(array.shape))
    spots = []
    for shift in (0, 1):
        where = [jax.random.randint(jax.random.fold_in(own_key, axis), (), 0, length) for axis, length in enumerate(array.shape)]
        where[longest] = (where[longest] + shift) % array.shape[longest]
        spots.append(tuple(where))
    return array.at[spots[0]].set(smallest).at[spots[1]].set(top_value)


def steps_of(own_key, shape, cuts, smallest, largest):
    gain = 1.0
    for axis_at, parts in cuts:
        steps = jax.random.uniform(jax.random.fold_in(jax.random.fold_in(own_key, 6), axis_at), (parts,), jnp.float32, smallest / len(cuts), largest / len(cuts))
        gain = gain * jnp.repeat(jnp.exp(steps), shape[axis_at] // parts).reshape((-1,) + (1,) * (len(shape) - 1 - axis_at))
    return gain


def scatter_about(rng, extent, scale, most, cuts=(), kind=jnp.bfloat16):
    level = steps_of(rng, extent, cuts, -0.22, 0.18) if cuts else 1.0
    drawn = jax.random.normal(rng, extent, jnp.float32) * scale * level
    return jnp.minimum(jnp.maximum(drawn, -most), most).astype(kind)


def setup_inputs(seed: int = 0) -> dict:
    key_of = jax.random.split(jax.random.key(seed), 12)
    initial_rates = jnp.clip(jax.random.uniform(key_of[0], (AREAS, UNITS, TRIALS), jnp.float32, -0.9, 0.9) * steps_of(key_of[0], (AREAS, UNITS, TRIALS), ((0, 32), (1, 8)), -0.4, 0.0), -0.9, 0.9)
    prior_rates = jnp.clip(jax.random.uniform(key_of[1], (AREAS, UNITS, TRIALS), jnp.float32, -0.8984375, 0.8984375) * steps_of(key_of[1], (AREAS, UNITS, TRIALS), ((0, 32), (1, 8)), -0.4, 0.0), -0.8984375, 0.8984375).astype(jnp.bfloat16)
    local_weight = scatter_about(key_of[2], (AREAS, UNITS, UNITS), (UNITS // 2) ** -0.5, 0.125, ((0, 32), (1, 8)))
    long_weight = scatter_about(key_of[3], (AREAS, UNITS, INPUTS), (INPUTS // 2) ** -0.5, 0.1875, ((0, 32), (1, 8)))
    input_weight = scatter_about(key_of[4], (AREAS, UNITS, STIM), STIM ** -0.5, 1.5, ((0, 32), (1, 8)))
    unit_bias = scatter_about(key_of[5], (AREAS, UNITS), 0.3, 2.5, ((0, 32), (1, 8)), jnp.float32)
    leak_rate = jnp.clip(jnp.exp(math.log(1.0) - 1.609438 * jax.random.uniform(key_of[6], (AREAS, UNITS), jnp.float32) ** steps_of(key_of[6], (AREAS, UNITS), ((0, 32), (1, 8)), -0.2, 0.2)), 0.2, 1.0)
    stimulus = scatter_about(key_of[7], (STEPS, STIM, TRIALS), 1.0, 4.0)
    link_source = draw_link_source(jax.random.fold_in(key_of[11], 71), 0)
    link_block = with_ends(jax.random.randint(key_of[9], (AREAS, SLOTS), 0, UNITS // BLOCK), jax.random.fold_in(key_of[9], 1), 0, (UNITS // BLOCK) - 1).astype(jnp.int32)
    link_delay = with_ends(jax.random.randint(key_of[10], (AREAS, SLOTS), 0, 2), jax.random.fold_in(key_of[10], 1), 0, 1).astype(jnp.int32)
    return dict(initial_rates=initial_rates, prior_rates=prior_rates, local_weight=local_weight, long_weight=long_weight, input_weight=input_weight, unit_bias=unit_bias, leak_rate=leak_rate, stimulus=stimulus, link_source=link_source, link_block=link_block, link_delay=link_delay)


def per_area(weights, factors):
    return lax.map(lambda operands: jnp.dot(operands[0], operands[1], preferred_element_type=jnp.float32), (weights, factors))


def pick_inputs(earlier, later_copy, link_source, link_block, link_delay):
    block_count = UNITS // BLOCK
    history = jnp.stack([later_copy, earlier], axis=1).reshape(AREAS, 2 * block_count, BLOCK, TRIALS)
    flat_rows = (link_delay * block_count + link_block).astype(jnp.int32)
    picked = history[link_source.astype(jnp.int32), flat_rows]
    return picked.reshape(AREAS, SLOTS * BLOCK, TRIALS)


def update(state_now, copy_now, current, stim_now, local_weight, input_weight, unit_bias, leak_rate):
    drive_sum = per_area(local_weight, copy_now) + current
    drive_sum = drive_sum + jnp.einsum("aus,st->aut", input_weight.astype(jnp.float32), stim_now.astype(jnp.float32))
    drive_sum = drive_sum + unit_bias[:, :, None]
    return state_now + leak_rate[:, :, None] * (jnp.tanh(drive_sum) - state_now)


def reference(initial_rates, prior_rates, local_weight, long_weight, input_weight, unit_bias, leak_rate, stimulus, link_source, link_block, link_delay):
    state_now = initial_rates
    later_copy = initial_rates.astype(jnp.bfloat16)
    earlier = prior_rates
    for window in range(WINDOWS):
        current = per_area(long_weight, pick_inputs(earlier, later_copy, link_source, link_block, link_delay))
        state_now = update(state_now, later_copy, current, stimulus[2 * window], local_weight, input_weight, unit_bias, leak_rate)
        earlier = state_now.astype(jnp.bfloat16)
        state_now = update(state_now, earlier, current, stimulus[2 * window + 1], local_weight, input_weight, unit_bias, leak_rate)
        later_copy = state_now.astype(jnp.bfloat16)
    final_current = per_area(long_weight, pick_inputs(earlier, later_copy, link_source, link_block, link_delay))
    return state_now, final_current
```

```python
import functools

import jax
import jax.numpy as jnp
from jax import lax
from jax.experimental import pallas as pl
from jax.experimental.pallas import tpu as pltpu
from jax.sharding import PartitionSpec as P

UNITS = 4096
BLOCK = 128
WINDOWS = 3
ROWS = 512
HALF = BLOCK // 2
BLOCKS = UNITS // BLOCK


VMEM = pl.BlockSpec(memory_space=pltpu.VMEM)
SMEM = pl.BlockSpec(memory_space=pltpu.SMEM)
F32 = jnp.float32
BF16 = jnp.bfloat16

SRC, PIECE, CORE = 32, 48, 56


def assemble(table, pieces, full):
    for m, piece in enumerate(pieces):
        start = pl.multiple_of(table[PIECE + m], ROWS)
        full[pl.ds(start, ROWS), :] = piece[...]


def select_kernel(table, *refs):
    *pieces, earlier, full, outgoing = refs
    assemble(table, pieces, full)
    send(table, full, earlier, outgoing)


def send(table, later, earlier, outgoing):
    half = table[CORE] * HALF

    def one(area, carry):
        row = table[area]
        is_later = row < BLOCKS
        start = pl.multiple_of(jnp.where(is_later, row, row - BLOCKS) * BLOCK + half, HALF)

        @pl.when(is_later)
        def _():
            outgoing[area] = later[pl.ds(start, HALF), :]

        @pl.when(jnp.logical_not(is_later))
        def _():
            outgoing[area] = earlier[pl.ds(start, HALF), :]

        return carry

    lax.fori_loop(0, BLOCKS, one, 0, unroll=4)


def local_kernel(weight, full, drive, out):
    out[...] = drive[...] + jnp.dot(weight[...], full[...], preferred_element_type=F32)


def collect(table, mine, theirs, inputs):
    half = pl.multiple_of(table[CORE] * HALF, HALF)
    other = pl.multiple_of(HALF - half, HALF)
    for slot in range(16):
        area = table[SRC + slot]
        inputs[pl.ds(slot * BLOCK + half, HALF), :] = mine[area]
        inputs[pl.ds(slot * BLOCK + other, HALF), :] = theirs[area]


def current_kernel(table, weight, mine, theirs, current, inputs):
    collect(table, mine, theirs, inputs)
    current[...] = jnp.dot(weight[...], inputs[...], preferred_element_type=F32)


def moved(rates, leak, drive):
    return rates + leak * (jnp.tanh(drive) - rates)


def first_kernel(table, weight, mine, theirs, partial, rates, leak, current, out, copy, inputs):
    collect(table, mine, theirs, inputs)
    now = jnp.dot(weight[...], inputs[...], preferred_element_type=F32)
    current[...] = now
    new = moved(rates[...], leak[...], partial[...] + now)
    out[...] = new
    copy[...] = new.astype(BF16)


def second_kernel(table, weight, *refs):
    *pieces, current, drive, rates, leak, full, out, copy = refs
    assemble(table, pieces, full)
    total = jnp.dot(weight[...], full[...], preferred_element_type=F32) + current[...] + drive[...]
    new = moved(rates[...], leak[...], total)
    out[...] = new
    copy[...] = new.astype(BF16)


def assemble_kernel(table, *refs):
    *pieces, full = refs
    assemble(table, pieces, full)


def call(kernel, name, inputs, outs, flops, scratch=()):
    byte_count = sum(x.size * x.dtype.itemsize for x in inputs)
    return pl.pallas_call(
        kernel,
        name=name,
        out_shape=outs,
        in_specs=[SMEM if x.dtype == jnp.int32 else VMEM for x in inputs],
        out_specs=jax.tree.map(lambda _: VMEM, outs),
        scratch_shapes=list(scratch),
        cost_estimate=pl.CostEstimate(flops=flops, bytes_accessed=byte_count, transcendentals=0),
        compiler_params=pltpu.CompilerParams(vmem_limit_bytes=24 * 2**20),
    )(*inputs)


def shape(rows, dtype):
    return jax.ShapeDtypeStruct((rows, BLOCK), dtype)


def exchange(piece):
    def swapped(x):
        return lax.ppermute(x, "unit", [(u, u ^ 1) for u in range(8)])

    near = [lax.ppermute(piece, "unit", [(u, u ^ m) for u in range(8)]) for m in (2, 6, 4)]
    pieces = [piece, swapped(piece)]
    pieces += [near[0], swapped(near[0]), near[2], swapped(near[2]), near[1], swapped(near[1])]
    return pieces


def shards(
    initial_rates,
    prior_rates,
    local_weight,
    long_weight,
    input_weight,
    unit_bias,
    leak_rate,
    stimulus,
    link_source,
    link_block,
    link_delay,
):
    area_here = lax.axis_index("area")
    unit_here = lax.axis_index("unit")
    block_row = link_delay * BLOCKS + link_block
    from_here = link_source == area_here
    send_rows = jnp.sum(jnp.where(from_here, block_row, 0), axis=1)
    own_source = lax.dynamic_index_in_dim(link_source, area_here, 0, keepdims=False)
    starts = (unit_here ^ jnp.arange(8, dtype=jnp.int32)) * ROWS
    core = jnp.full((8,), unit_here % 2, jnp.int32)
    table = jnp.concatenate([send_rows, own_source, starts, core]).astype(jnp.int32)
    weight_local = local_weight[0]
    weight_long = long_weight[0]
    leak = leak_rate[0][:, None]
    drives = jnp.einsum("us,nst->nut", input_weight[0], stimulus, preferred_element_type=F32)
    drives = drives + unit_bias[0][None, :, None]

    def long_range(outgoing):
        arrived = lax.all_to_all(outgoing, "area", split_axis=0, concat_axis=0, tiled=True)
        other = lax.ppermute(arrived, "unit", [(u, u ^ 1) for u in range(8)])
        return arrived, other

    def select(pieces, earlier):
        return call(
            select_kernel,
            "select",
            [table, *pieces, earlier],
            (shape(UNITS, BF16), jax.ShapeDtypeStruct((BLOCKS, HALF, BLOCK), BF16)),
            1000,
        )

    rates = initial_rates[0]
    gather_scratch = [pltpu.VMEM((16 * BLOCK, BLOCK), BF16)]
    earlier = call(assemble_kernel, "assemble", [table, *exchange(prior_rates[0])], shape(UNITS, BF16), 1000)
    later, outgoing = select(exchange(rates.astype(BF16)), earlier)
    for window in range(WINDOWS):
        mine, theirs = long_range(outgoing)
        partial = call(
            local_kernel, "local", [weight_local, later, drives[2 * window]], shape(ROWS, F32), 2 * ROWS * UNITS * BLOCK
        )
        current, rates, copy = call(
            first_kernel,
            "first",
            [table, weight_long, mine, theirs, partial, rates, leak],
            (shape(ROWS, F32), shape(ROWS, F32), shape(ROWS, BF16)),
            ROWS * UNITS * BLOCK,
            gather_scratch,
        )
        earlier, rates, copy = call(
            second_kernel,
            "second",
            [table, weight_local, *exchange(copy), current, drives[2 * window + 1], rates, leak],
            (shape(UNITS, BF16), shape(ROWS, F32), shape(ROWS, BF16)),
            2 * ROWS * UNITS * BLOCK,
        )
        later, outgoing = select(exchange(copy), earlier)
    mine, theirs = long_range(outgoing)
    final_current = call(
        current_kernel,
        "current",
        [table, weight_long, mine, theirs],
        shape(ROWS, F32),
        ROWS * UNITS * BLOCK,
        gather_scratch,
    )
    return (rates[None], final_current[None])


def solution(mesh):
    return jax.shard_map(
        shards,
        mesh=mesh,
        in_specs=(
            P("area", "unit", None),
            P("area", "unit", None),
            P("area", "unit", None),
            P("area", "unit", None),
            P("area", "unit", None),
            P("area", "unit"),
            P("area", "unit"),
            P(),
            P(),
            P(),
            P(),
        ),
        out_specs=(P("area", "unit", None), P("area", "unit", None)),
        check_vma=False,
    )
```

```python
import jax
import jax.numpy as jnp
from jax import lax
from jax.experimental import pallas as pl
from jax.experimental.pallas import tpu as pltpu
from jax.sharding import PartitionSpec as P


UNITS = 4096
BLOCK = 128
WINDOWS = 3
ROWS = 512
HALF = BLOCK // 2
BLOCKS = UNITS // BLOCK


VMEM = pl.BlockSpec(memory_space=pltpu.VMEM)
SMEM = pl.BlockSpec(memory_space=pltpu.SMEM)
F32 = jnp.float32
BF16 = jnp.bfloat16

SRC, CORE, UNIT = 32, 48, 56


def put(pieces, first, full):
    for m, piece in enumerate(pieces):
        full[(first + m) * ROWS : (first + m + 1) * ROWS, :] = piece[...]


def put_own(table, piece, pair, full):
    other = pl.multiple_of((1 - table[CORE]) * ROWS, ROWS)
    full[0:ROWS, :] = piece[...]
    full[ROWS : 2 * ROWS, :] = pair[pl.ds(other, ROWS), :]


def by_rows(work):
    def one(i, carry):
        work(pl.ds(pl.multiple_of(i * (ROWS // 2), ROWS // 2), ROWS // 2))
        return carry

    lax.fori_loop(0, 2, one, 0)


def send(table, sources, outgoing):
    half = table[CORE] * HALF

    def one(area, carry):
        row = table[area]
        for array, first in sources:
            count = array.shape[0] // BLOCK

            @pl.when((row >= first) & (row < first + count))
            def _():
                start = pl.multiple_of((row - first) * BLOCK + half, HALF)
                outgoing[area] = array[pl.ds(start, HALF), :]

        return carry

    lax.fori_loop(0, BLOCKS, one, 0, unroll=4)


def product(table, weight, rows, full, first):
    total = None
    for m in range(full.shape[0] // ROWS):
        columns = pl.ds(pl.multiple_of(table[UNIT + first + m], ROWS), ROWS)
        part = jnp.dot(weight[rows, columns], full[m * ROWS : (m + 1) * ROWS, :], preferred_element_type=F32)
        total = part if total is None else total + part
    return total


def begin_kernel(table, piece, pair, near, near_other, earlier, front, outgoing):
    put_own(table, piece, pair, front)
    put((near, near_other), 2, front)
    send(table, ((front, 0), (earlier, BLOCKS)), outgoing)


def finish_kernel(table, *refs):
    *pieces, begun, back, outgoing = refs
    del begun
    put(pieces, 0, back)
    send(table, ((back, BLOCKS // 2),), outgoing)


def start_kernel(table, own, other, near, far, far_other, second, front, back, outgoing, earlier):
    mine = pl.multiple_of(table[CORE] * 2 * ROWS, 2 * ROWS)
    theirs = pl.multiple_of(2 * ROWS - mine, 2 * ROWS)
    for m, (piece, row) in enumerate(
        ((own, 0), (other, 0), (near, mine), (near, theirs), (far, 0), (far_other, 0), (second, mine), (second, theirs))
    ):
        full, first = (front, m * ROWS) if m < 4 else (back, (m - 4) * ROWS)
        full[first : first + ROWS, :] = piece[pl.ds(row, ROWS), :]
        earlier[m * ROWS : (m + 1) * ROWS, :] = piece[pl.ds(row + ROWS, ROWS), :]
    send(table, ((front, 0), (back, BLOCKS // 2), (earlier, BLOCKS)), outgoing)


def local_kernel(table, weight, front, back, drive, out):
    @by_rows
    def _(rows):
        total = product(table, weight, rows, front, 0) + product(table, weight, rows, back, 4)
        out[rows, :] = drive[rows, :] + total


def collect(table, mine, theirs, inputs):
    half = pl.multiple_of(table[CORE] * HALF, HALF)
    other = pl.multiple_of(HALF - half, HALF)
    for slot in range(16):
        area = table[SRC + slot]
        inputs[pl.ds(slot * BLOCK + half, HALF), :] = mine[area]
        inputs[pl.ds(slot * BLOCK + other, HALF), :] = theirs[area]


def current_kernel(table, weight, mine, theirs, current, inputs):
    collect(table, mine, theirs, inputs)

    @by_rows
    def _(rows):
        current[rows, :] = jnp.dot(weight[rows, :], inputs[...], preferred_element_type=F32)


def moved(rates, leak, drive):
    return rates + leak * (jnp.tanh(drive) - rates)


def first_kernel(table, weight, mine, theirs, partial, rates, leak, current, out, copy, inputs):
    collect(table, mine, theirs, inputs)

    @by_rows
    def _(rows):
        now = jnp.dot(weight[rows, :], inputs[...], preferred_element_type=F32)
        current[rows, :] = now
        new = moved(rates[rows, :], leak[rows, :], partial[rows, :] + now)
        out[rows, :] = new
        copy[rows, :] = new.astype(BF16)


def early_kernel(table, weight, piece, pair, *refs):
    *pieces, current, drive, out, full = refs
    put_own(table, piece, pair, full)
    put(pieces, 2, full)

    @by_rows
    def _(rows):
        total = product(table, weight, rows, full, 0)
        out[rows, :] = current[rows, :] + drive[rows, :] + total


def second_kernel(table, weight, *refs):
    *pieces, before, partial, rates, leak, full, out, copy = refs
    size = before.shape[0]
    full[0:size, :] = before[...]
    put(pieces, size // ROWS, full)

    @by_rows
    def _(rows):
        total = product(table, weight, rows, full.at[pl.ds(size, UNITS - size), :], size // ROWS)
        new = moved(rates[rows, :], leak[rows, :], partial[rows, :] + total)
        out[rows, :] = new
        copy[rows, :] = new.astype(BF16)


def drive_kernel(weight, stimulus, bias, leak, local_weight, out, leak_out):
    del local_weight
    leak_out[...] = leak[...]

    def one(n, carry):
        part = lax.dot_general(weight[...], stimulus[n], (((0,), (0,)), ((), ())), preferred_element_type=F32)
        out[n] = part + bias[...]
        return carry

    lax.fori_loop(0, 2 * WINDOWS, one, 0)


def both_kernel(rates, prior, out):
    out[0:ROWS, :] = rates[...].astype(BF16)
    out[ROWS : 2 * ROWS, :] = prior[...]


def call(kernel, inputs, outs, flops, scratch=(), aliases=None):
    byte_count = sum(x.size * x.dtype.itemsize for x in inputs)
    return pl.pallas_call(
        kernel,
        out_shape=outs,
        in_specs=[SMEM if x.dtype == jnp.int32 else VMEM for x in inputs],
        out_specs=jax.tree.map(lambda _: VMEM, outs),
        scratch_shapes=list(scratch),
        input_output_aliases=aliases or {},
        cost_estimate=pl.CostEstimate(flops=flops, bytes_accessed=byte_count, transcendentals=0),
        compiler_params=pltpu.CompilerParams(vmem_limit_bytes=24 * 2**20),
    )(*inputs)


def shape(rows, dtype):
    return jax.ShapeDtypeStruct((rows, BLOCK), dtype)


def paired(piece):
    return lax.all_gather(piece, "unit", axis=0, tiled=True, axis_index_groups=[[0, 1], [2, 3], [4, 5], [6, 7]])


PAIRS = [(u, u ^ 1) for u in range(8)]


def neighbours(piece):
    found = []
    for m in (2, 6, 4):
        found.append(lax.ppermute(piece, "unit", [(u, u ^ m) for u in range(8)]))
    return found


def exchange(piece):
    near, second, far = neighbours(piece)
    near, pair = lax.optimization_barrier((near, paired(piece)))
    pieces = [piece, pair]
    for x in (near, far, second):
        pieces += [x, lax.ppermute(x, "unit", PAIRS)]
    return pieces


def shards(
    initial_rates,
    prior_rates,
    local_weight,
    long_weight,
    input_weight,
    unit_bias,
    leak_rate,
    stimulus,
    link_source,
    link_block,
    link_delay,
):
    area_here = lax.axis_index("area")
    unit_here = lax.axis_index("unit")
    order = unit_here ^ jnp.arange(8, dtype=jnp.int32)
    place = link_block ^ (unit_here * (ROWS // BLOCK))
    block_row = link_delay * BLOCKS + place
    from_here = link_source == area_here
    send_rows = jnp.sum(jnp.where(from_here, block_row, 0), axis=1)
    own_source = lax.dynamic_index_in_dim(link_source, area_here, 0, keepdims=False)
    core = jnp.full((8,), unit_here % 2, jnp.int32)
    table = jnp.concatenate([send_rows, own_source, core, order * ROWS]).astype(jnp.int32)
    weight_local = local_weight[0]
    weight_long = long_weight[0]
    drives, leak = call(
        drive_kernel,
        [input_weight[0].T, stimulus, unit_bias[0][:, None], leak_rate[0][:, None], weight_local],
        (jax.ShapeDtypeStruct((2 * WINDOWS, ROWS, BLOCK), F32), jax.ShapeDtypeStruct((ROWS, 1), F32)),
        1000,
    )
    flops = ROWS * UNITS * BLOCK

    def long_range(outgoing):
        arrived = lax.all_to_all(outgoing, "area", split_axis=0, concat_axis=0, tiled=True)
        other = lax.ppermute(arrived, "unit", [(u, u ^ 1) for u in range(8)])
        return arrived, other

    gather_scratch = [pltpu.VMEM((16 * BLOCK, BLOCK), BF16)]
    history = shape(UNITS, BF16)
    parcels = jax.ShapeDtypeStruct((BLOCKS, HALF, BLOCK), BF16)
    half_history = shape(UNITS // 2, BF16)
    both = call(both_kernel, [initial_rates[0], prior_rates[0]], shape(2 * ROWS, BF16), 1000)
    near, second, far = neighbours(both)
    other = lax.ppermute(both, "unit", PAIRS)
    far, drives, leak = lax.optimization_barrier((far, drives, leak))
    pairs = [both, other, paired(near), far, lax.ppermute(far, "unit", PAIRS), paired(second)]
    *later, outgoing = call(
        start_kernel, [table, *pairs], (half_history, half_history, parcels), 1000, [pltpu.VMEM((UNITS, BLOCK), BF16)]
    )

    def window(step, carry):
        later, outgoing, rates = carry
        mine, theirs = long_range(outgoing)
        drive = [drives[2 * step + n] for n in range(2)]
        partial = call(local_kernel, [table, weight_local, *later, drive[0]], shape(ROWS, F32), 2 * flops)
        current, rates, copy = call(
            first_kernel,
            [table, weight_long, mine, theirs, partial, rates, leak],
            (shape(ROWS, F32), shape(ROWS, F32), shape(ROWS, BF16)),
            flops,
            gather_scratch,
        )
        pieces = exchange(copy)
        partial, before = call(
            early_kernel,
            [table, weight_local, *pieces[:4], current, drive[1]],
            (shape(ROWS, F32), shape(4 * ROWS, BF16)),
            flops,
        )
        earlier, rates, copy = call(
            second_kernel,
            [table, weight_local, *pieces[4:], before, partial, rates, leak],
            (history, shape(ROWS, F32), shape(ROWS, BF16)),
            flops,
        )
        pieces = exchange(copy)
        front, outgoing = call(begin_kernel, [table, *pieces[:4], earlier], (half_history, parcels), 1000)
        back, outgoing = call(
            finish_kernel, [table, *pieces[4:], outgoing], (half_history, parcels), 1000, aliases={5: 1}
        )
        later = [front, back]
        return later, outgoing, rates

    carry = (later, outgoing, initial_rates[0])
    for step in range(WINDOWS):
        carry = window(step, carry)
    later, outgoing, rates = carry
    mine, theirs = long_range(outgoing)
    final_current = call(current_kernel, [table, weight_long, mine, theirs], shape(ROWS, F32), flops, gather_scratch)
    return (rates[None], final_current[None])


def solution(mesh):
    return jax.shard_map(
        shards,
        mesh=mesh,
        in_specs=(
            P("area", "unit", None),
            P("area", "unit", None),
            P("area", "unit", None),
            P("area", "unit", None),
            P("area", "unit", None),
            P("area", "unit"),
            P("area", "unit"),
            P(),
            P(),
            P(),
            P(),
        ),
        out_specs=(P("area", "unit", None), P("area", "unit", None)),
        check_vma=False,
    )
```

```python
import jax
import jax.numpy as jnp
from jax import lax
from jax.experimental import pallas as pl
from jax.experimental.pallas import tpu as pltpu
from jax.sharding import PartitionSpec as P


UNITS = 4096
BLOCK = 128
WINDOWS = 3
ROWS = 512
HALF = BLOCK // 2
BLOCKS = UNITS // BLOCK


VMEM = pl.BlockSpec(memory_space=pltpu.VMEM)
SMEM = pl.BlockSpec(memory_space=pltpu.SMEM)
F32 = jnp.float32
BF16 = jnp.bfloat16

SRC, CORE, UNIT = 32, 48, 56


def put(pieces, first, full):
    for m, piece in enumerate(pieces):
        full[(first + m) * ROWS : (first + m + 1) * ROWS, :] = piece[...]


def put_own(table, piece, pair, full):
    other = pl.multiple_of((1 - table[CORE]) * ROWS, ROWS)
    full[0:ROWS, :] = piece[...]
    full[ROWS : 2 * ROWS, :] = pair[pl.ds(other, ROWS), :]


def by_rows(work):
    def one(i, carry):
        work(pl.ds(pl.multiple_of(i * (ROWS // 2), ROWS // 2), ROWS // 2))
        return carry

    lax.fori_loop(0, 2, one, 0)


def send(table, lists, counts, stage, sources, outgoing):
    half = table[CORE] * HALF

    def one(i, carry):
        area = lists[stage, i]
        row = table[area]
        for array, first in sources:
            count = array.shape[0] // BLOCK

            @pl.when((row >= first) & (row < first + count))
            def _():
                start = pl.multiple_of((row - first) * BLOCK + half, HALF)
                outgoing[area] = array[pl.ds(start, HALF), :]

        return carry

    lax.fori_loop(0, counts[stage], one, 0)


def product(table, weight, rows, full, first):
    total = None
    for m in range(full.shape[0] // ROWS):
        columns = pl.ds(pl.multiple_of(table[UNIT + first + m] * ROWS, ROWS), ROWS)
        part = jnp.dot(weight[rows, columns], full[m * ROWS : (m + 1) * ROWS, :], preferred_element_type=F32)
        total = part if total is None else total + part
    return total


def begin_kernel(table, lists, counts, piece, pair, near, near_other, earlier, front, outgoing):
    put_own(table, piece, pair, front)
    put((near, near_other), 2, front)
    send(table, lists, counts, 0, ((front, 0), (earlier, BLOCKS)), outgoing)


def finish_kernel(table, lists, counts, *refs):
    *pieces, begun, back, outgoing = refs
    del begun
    put(pieces, 0, back)
    send(table, lists, counts, 1, ((back, BLOCKS // 2),), outgoing)


def last_begin_kernel(*refs):
    *inputs, outgoing, front = refs
    begin_kernel(*inputs, front, outgoing)


def last_finish_kernel(*refs):
    *inputs, outgoing, back = refs
    finish_kernel(*inputs, back, outgoing)


def copy_kernel(source, out):
    out[...] = source[...]


def start_kernel(table, lists, counts, own, near, far, far_other, second, front, back, outgoing, earlier):
    mine = pl.multiple_of(table[CORE] * 2 * ROWS, 2 * ROWS)
    theirs = pl.multiple_of(2 * ROWS - mine, 2 * ROWS)
    for m, (piece, row) in enumerate(
        ((own, mine), (own, theirs), (near, mine), (near, theirs), (far, 0), (far_other, 0), (second, mine), (second, theirs))
    ):
        full, first = (front, m * ROWS) if m < 4 else (back, (m - 4) * ROWS)
        full[first : first + ROWS, :] = piece[pl.ds(row, ROWS), :]
        earlier[m * ROWS : (m + 1) * ROWS, :] = piece[pl.ds(row + ROWS, ROWS), :]
    send(table, lists, counts, 0, ((front, 0), (earlier, BLOCKS)), outgoing)
    send(table, lists, counts, 1, ((back, BLOCKS // 2),), outgoing)


def local_kernel(table, weight, front, back, drive, out):
    @by_rows
    def _(rows):
        total = product(table, weight, rows, front, 0) + product(table, weight, rows, back, 4)
        out[rows, :] = drive[rows, :] + total


def collect(table, mine, theirs, inputs):
    half = pl.multiple_of(table[CORE] * HALF, HALF)
    other = pl.multiple_of(HALF - half, HALF)
    for slot in range(16):
        area = table[SRC + slot]
        inputs[pl.ds(slot * BLOCK + half, HALF), :] = mine[area]
        inputs[pl.ds(slot * BLOCK + other, HALF), :] = theirs[area]


def current_kernel(table, weight, mine, theirs, current, inputs):
    collect(table, mine, theirs, inputs)

    @by_rows
    def _(rows):
        current[rows, :] = jnp.dot(weight[rows, :], inputs[...], preferred_element_type=F32)


def moved(rates, leak, drive):
    return rates + leak * (jnp.tanh(drive) - rates)


def first_kernel(table, weight, mine, theirs, partial, rates, leak, current, out, copy, inputs):
    collect(table, mine, theirs, inputs)

    @by_rows
    def _(rows):
        now = jnp.dot(weight[rows, :], inputs[...], preferred_element_type=F32)
        current[rows, :] = now
        new = moved(rates[rows, :], leak[rows, :], partial[rows, :] + now)
        out[rows, :] = new
        copy[rows, :] = new.astype(BF16)


def early_kernel(table, weight, piece, pair, *refs):
    *pieces, current, drive, out, full = refs
    put_own(table, piece, pair, full)
    put(pieces, 2, full)

    @by_rows
    def _(rows):
        total = product(table, weight, rows, full, 0)
        out[rows, :] = current[rows, :] + drive[rows, :] + total


def second_kernel(table, weight, *refs):
    *pieces, before, partial, rates, leak, full, out, copy = refs
    size = before.shape[0]
    full[0:size, :] = before[...]
    put(pieces, size // ROWS, full)

    @by_rows
    def _(rows):
        total = product(table, weight, rows, full.at[pl.ds(size, UNITS - size), :], size // ROWS)
        new = moved(rates[rows, :], leak[rows, :], partial[rows, :] + total)
        out[rows, :] = new
        copy[rows, :] = new.astype(BF16)


def column(row):
    return jnp.transpose(jnp.broadcast_to(row, (BLOCK, row.shape[1])))


def drive_kernel(weight, stimulus, bias, leak, local_weight, out, leak_out):
    del local_weight
    leak_out[...] = column(leak[...])
    base = column(bias[...])

    def one(n, carry):
        part = lax.dot_general(weight[...], stimulus[n], (((0,), (0,)), ((), ())), preferred_element_type=F32)
        out[n] = part + base
        return carry

    lax.fori_loop(0, 2 * WINDOWS, one, 0)


def both_kernel(rates, prior, out):
    out[0:ROWS, :] = rates[...].astype(BF16)
    out[ROWS : 2 * ROWS, :] = prior[...]


def call(kernel, inputs, outs, flops, scratch=(), aliases=None):
    byte_count = sum(x.size * x.dtype.itemsize for x in inputs)
    return pl.pallas_call(
        kernel,
        out_shape=outs,
        in_specs=[SMEM if x.dtype == jnp.int32 else VMEM for x in inputs],
        out_specs=jax.tree.map(lambda _: VMEM, outs),
        scratch_shapes=list(scratch),
        input_output_aliases=aliases or {},
        cost_estimate=pl.CostEstimate(flops=flops, bytes_accessed=byte_count, transcendentals=0),
        compiler_params=pltpu.CompilerParams(vmem_limit_bytes=24 * 2**20),
    )(*inputs)


def shape(rows, dtype):
    return jax.ShapeDtypeStruct((rows, BLOCK), dtype)


def paired(piece):
    return lax.all_gather(piece, "unit", axis=0, tiled=True, axis_index_groups=[[0, 1], [2, 3], [4, 5], [6, 7]])


PAIRS = [(u, u ^ 1) for u in range(8)]


def neighbours(piece):
    found = []
    for m in (2, 6, 4):
        found.append(lax.ppermute(piece, "unit", [(u, u ^ m) for u in range(8)]))
    return found


def exchange(piece):
    near, second, far = neighbours(piece)
    near, pair = lax.optimization_barrier((near, paired(piece)))
    pieces = [piece, pair]
    for x in (near, far, second):
        pieces += [x, lax.ppermute(x, "unit", PAIRS)]
    return pieces


def shards(
    initial_rates,
    prior_rates,
    local_weight,
    long_weight,
    input_weight,
    unit_bias,
    leak_rate,
    stimulus,
    link_source,
    link_block,
    link_delay,
):
    area_here = lax.axis_index("area")
    unit_here = lax.axis_index("unit")
    order = unit_here ^ jnp.arange(8, dtype=jnp.int32)
    place = link_block ^ (unit_here * (ROWS // BLOCK))
    block_row = link_delay * BLOCKS + place
    from_here = link_source == area_here
    send_rows = jnp.sum(jnp.where(from_here, block_row, 0), axis=1)
    own_source = lax.dynamic_index_in_dim(link_source, area_here, 0, keepdims=False)
    core = jnp.full((8,), unit_here % 2, jnp.int32)
    live = jnp.any(from_here, axis=1)
    late = (send_rows >= BLOCKS // 2) & (send_rows < BLOCKS)
    areas = jnp.arange(BLOCKS, dtype=jnp.int32)
    stages = jnp.arange(2, dtype=jnp.int32)
    chosen = live[None, :] & (late.astype(jnp.int32)[None, :] == stages[:, None])
    ahead = chosen[:, None, :] & (areas[None, None, :] < areas[None, :, None])
    place = jnp.sum(ahead.astype(jnp.int32), axis=2)
    here = chosen[:, None, :] & (place[:, None, :] == areas[None, :, None])
    lists = jnp.sum(jnp.where(here, areas[None, None, :], 0), axis=2).astype(jnp.int32)
    counts = jnp.sum(chosen.astype(jnp.int32), axis=1).astype(jnp.int32)
    table = jnp.concatenate([send_rows, own_source, core, order]).astype(jnp.int32)
    tables = [table, lists, counts]
    weight_local = local_weight[0]
    weight_long = long_weight[0]
    drives, leak = call(
        drive_kernel,
        [input_weight[0].T, stimulus, unit_bias, leak_rate, weight_local],
        (jax.ShapeDtypeStruct((2 * WINDOWS, ROWS, BLOCK), F32), shape(ROWS, F32)),
        1000,
    )
    flops = ROWS * UNITS * BLOCK

    def long_range(outgoing):
        arrived = lax.all_to_all(outgoing, "area", split_axis=0, concat_axis=0, tiled=True)
        other = lax.ppermute(arrived, "unit", PAIRS)
        return arrived, other

    gather_scratch = [pltpu.VMEM((16 * BLOCK, BLOCK), BF16)]
    history = shape(UNITS, BF16)
    parcels = jax.ShapeDtypeStruct((BLOCKS, HALF, BLOCK), BF16)
    half_history = shape(UNITS // 2, BF16)
    both = call(both_kernel, [initial_rates[0], prior_rates[0]], shape(2 * ROWS, BF16), 1000)
    near, second, far = neighbours(both)
    own = paired(both)
    far, drives, leak = lax.optimization_barrier((far, drives, leak))
    near = paired(near)
    pairs = [own, near, far, lax.ppermute(far, "unit", PAIRS), paired(second)]
    *later, outgoing = call(
        start_kernel, [*tables, *pairs], (half_history, half_history, parcels), 1000, [pltpu.VMEM((UNITS, BLOCK), BF16)]
    )

    def window(step, carry):
        later, outgoing, rates = carry
        mine, theirs = long_range(outgoing)
        drive = [drives[2 * step + n] for n in range(2)]
        partial = call(local_kernel, [table, weight_local, *later, drive[0]], shape(ROWS, F32), 2 * flops)
        current, rates, copy = call(
            first_kernel,
            [table, weight_long, mine, theirs, partial, rates, leak],
            (shape(ROWS, F32), shape(ROWS, F32), shape(ROWS, BF16)),
            flops,
            gather_scratch,
        )
        pieces = exchange(copy)
        partial, before = call(
            early_kernel,
            [table, weight_local, *pieces[:4], current, drive[1]],
            (shape(ROWS, F32), shape(4 * ROWS, BF16)),
            flops,
        )
        earlier, rates, copy = call(
            second_kernel,
            [table, weight_local, *pieces[4:], before, partial, rates, leak],
            (history, shape(ROWS, F32), shape(ROWS, BF16)),
            flops,
        )
        pieces = exchange(copy)
        if step == WINDOWS - 1:
            scratch = [pltpu.VMEM((UNITS // 2, BLOCK), BF16)]
            outgoing = call(last_begin_kernel, [*tables, *pieces[:4], earlier], parcels, 1000, scratch)
            inputs = [*tables, *pieces[4:], outgoing]
            return None, call(last_finish_kernel, inputs, parcels, 1000, scratch, {7: 0}), rates
        keep = ((half_history, parcels), 1000)
        front, outgoing = call(begin_kernel, [*tables, *pieces[:4], earlier], *keep)
        back, outgoing = call(finish_kernel, [*tables, *pieces[4:], outgoing], *keep, aliases={7: 1})
        later = [front, back]
        return later, outgoing, rates

    carry = (later, outgoing, initial_rates[0])
    for step in range(WINDOWS):
        carry = window(step, carry)
    later, outgoing, rates = carry
    mine, theirs = long_range(outgoing)
    rates = call(copy_kernel, [rates], shape(ROWS, F32), 1000)
    final_current = call(current_kernel, [table, weight_long, mine, theirs], shape(ROWS, F32), flops, gather_scratch)
    return (rates[None], final_current[None])


def solution(mesh):
    return jax.shard_map(
        shards,
        mesh=mesh,
        in_specs=(
            P("area", "unit", None),
            P("area", "unit", None),
            P("area", "unit", None),
            P("area", "unit", None),
            P("area", "unit", None),
            P("area", "unit"),
            P("area", "unit"),
            P(),
            P(),
            P(),
            P(),
        ),
        out_specs=(P("area", "unit", None), P("area", "unit", None)),
        check_vma=False,
    )
```

```python
import jax
import jax.numpy as jnp
from jax import lax
from jax.experimental import pallas as pl
from jax.experimental.pallas import tpu as pltpu
from jax.sharding import PartitionSpec as P


UNITS = 4096
BLOCK = 128
WINDOWS = 3
ROWS = 512
HALF = BLOCK // 2
BLOCKS = UNITS // BLOCK


VMEM = pl.BlockSpec(memory_space=pltpu.VMEM)
SMEM = pl.BlockSpec(memory_space=pltpu.SMEM)
HBM = pl.BlockSpec(memory_space=pltpu.HBM)
F32 = jnp.float32
BF16 = jnp.bfloat16

SRC, CORE, UNIT = 32, 48, 56


def put(pieces, first, full):
    for m, piece in enumerate(pieces):
        full[(first + m) * ROWS : (first + m + 1) * ROWS, :] = piece[...]


def put_own(table, piece, pair, full):
    other = pl.multiple_of((1 - table[CORE]) * ROWS, ROWS)
    full[0:ROWS, :] = piece[...]
    full[ROWS : 2 * ROWS, :] = pair[pl.ds(other, ROWS), :]


def by_rows(work):
    def one(i, carry):
        work(pl.ds(pl.multiple_of(i * (ROWS // 2), ROWS // 2), ROWS // 2))
        return carry

    lax.fori_loop(0, 2, one, 0)


def send(table, lists, counts, stage, sources, outgoing):
    half = table[CORE] * HALF

    def one(i, carry):
        area = lists[stage, i]
        row = table[area]
        for array, first in sources:
            count = array.shape[0] // BLOCK

            @pl.when((row >= first) & (row < first + count))
            def _():
                start = pl.multiple_of((row - first) * BLOCK + half, HALF)
                outgoing[area] = array[pl.ds(start, HALF), :]

        return carry

    lax.fori_loop(0, counts[stage], one, 0)


def product(table, weight, rows, full, first):
    total = None
    for m in range(full.shape[0] // ROWS):
        columns = pl.ds(pl.multiple_of(table[UNIT + first + m] * ROWS, ROWS), ROWS)
        part = jnp.dot(weight[rows, columns], full[m * ROWS : (m + 1) * ROWS, :], preferred_element_type=F32)
        total = part if total is None else total + part
    return total


def begin_kernel(table, lists, counts, piece, pair, near, near_other, earlier, front, outgoing):
    put_own(table, piece, pair, front)
    put((near, near_other), 2, front)
    send(table, lists, counts, 0, ((front, 0), (earlier, BLOCKS)), outgoing)


def finish_kernel(table, lists, counts, *refs):
    *pieces, begun, back, outgoing = refs
    del begun
    put(pieces, 0, back)
    send(table, lists, counts, 1, ((back, BLOCKS // 2),), outgoing)


def last_begin_kernel(*refs):
    *inputs, outgoing, front = refs
    begin_kernel(*inputs, front, outgoing)


def last_finish_kernel(*refs):
    *inputs, outgoing, back = refs
    finish_kernel(*inputs, back, outgoing)


def copy_kernel(source, out):
    out[...] = source[...]


def start_kernel(table, lists, counts, own, near, far, far_other, second, front, back, outgoing, earlier):
    mine = pl.multiple_of(table[CORE] * 2 * ROWS, 2 * ROWS)
    theirs = pl.multiple_of(2 * ROWS - mine, 2 * ROWS)
    for m, (piece, row) in enumerate(
        ((own, mine), (own, theirs), (near, mine), (near, theirs), (far, 0), (far_other, 0), (second, mine), (second, theirs))
    ):
        full, first = (front, m * ROWS) if m < 4 else (back, (m - 4) * ROWS)
        full[first : first + ROWS, :] = piece[pl.ds(row, ROWS), :]
        earlier[m * ROWS : (m + 1) * ROWS, :] = piece[pl.ds(row + ROWS, ROWS), :]
    send(table, lists, counts, 0, ((front, 0), (earlier, BLOCKS)), outgoing)
    send(table, lists, counts, 1, ((back, BLOCKS // 2),), outgoing)


def local_kernel(table, weight, front, back, drive, out):
    @by_rows
    def _(rows):
        total = product(table, weight, rows, front, 0) + product(table, weight, rows, back, 4)
        out[rows, :] = drive[rows, :] + total


def collect(table, mine, theirs, inputs):
    half = pl.multiple_of(table[CORE] * HALF, HALF)
    other = pl.multiple_of(HALF - half, HALF)
    for slot in range(16):
        area = table[SRC + slot]
        inputs[pl.ds(slot * BLOCK + half, HALF), :] = mine[area]
        inputs[pl.ds(slot * BLOCK + other, HALF), :] = theirs[area]


def current_kernel(table, weight, mine, theirs, current, inputs):
    collect(table, mine, theirs, inputs)

    @by_rows
    def _(rows):
        current[rows, :] = jnp.dot(weight[rows, :], inputs[...], preferred_element_type=F32)


def moved(rates, leak, drive):
    return rates + leak * (jnp.tanh(drive) - rates)


def first_kernel(table, weight, mine, theirs, partial, rates, leak, current, out, copy, inputs):
    collect(table, mine, theirs, inputs)

    @by_rows
    def _(rows):
        now = jnp.dot(weight[rows, :], inputs[...], preferred_element_type=F32)
        current[rows, :] = now
        new = moved(rates[rows, :], leak[rows, :], partial[rows, :] + now)
        out[rows, :] = new
        copy[rows, :] = new.astype(BF16)


def early_kernel(table, weight, piece, pair, *refs):
    *pieces, current, drive, out, full = refs
    put_own(table, piece, pair, full)
    put(pieces, 2, full)

    @by_rows
    def _(rows):
        total = product(table, weight, rows, full, 0)
        out[rows, :] = current[rows, :] + drive[rows, :] + total


def second_kernel(table, weight, *refs):
    *pieces, before, partial, rates, leak, full, out, copy = refs
    size = before.shape[0]
    full[0:size, :] = before[...]
    put(pieces, size // ROWS, full)

    @by_rows
    def _(rows):
        total = product(table, weight, rows, full.at[pl.ds(size, UNITS - size), :], size // ROWS)
        new = moved(rates[rows, :], leak[rows, :], partial[rows, :] + total)
        out[rows, :] = new
        copy[rows, :] = new.astype(BF16)


def column(row):
    return jnp.transpose(jnp.broadcast_to(row, (BLOCK, row.shape[1])))


def fetch(sources, places, done):
    copies = [pltpu.make_async_copy(x, y, done.at[i]) for i, (x, y) in enumerate(zip(sources, places))]
    for copy in copies:
        copy.start()
    for copy in copies:
        copy.wait()


def drive_kernel(*refs):
    out, leak_out, weight, stimulus, bias, leak, done = refs[-7:]
    fetch(refs[:4], (weight, stimulus, bias, leak), done)
    leak_out[...] = column(leak[...])
    base = column(bias[...])

    def one(n, carry):
        part = lax.dot_general(weight[...], stimulus[n], (((0,), (0,)), ((), ())), preferred_element_type=F32)
        out[n] = part + base
        return carry

    lax.fori_loop(0, 2 * WINDOWS, one, 0)


def both_kernel(rates, prior, out, rates_here, done):
    fetch((rates, prior), (rates_here, out.at[ROWS : 2 * ROWS, :]), done)
    out[0:ROWS, :] = rates_here[...].astype(BF16)


def call(kernel, inputs, outs, flops, scratch=(), aliases=None, far=0):
    byte_count = sum(x.size * x.dtype.itemsize for x in inputs)
    return pl.pallas_call(
        kernel,
        out_shape=outs,
        in_specs=[HBM if i < far else SMEM if x.dtype == jnp.int32 else VMEM for i, x in enumerate(inputs)],
        out_specs=jax.tree.map(lambda _: VMEM, outs),
        scratch_shapes=list(scratch),
        input_output_aliases=aliases or {},
        cost_estimate=pl.CostEstimate(flops=flops, bytes_accessed=byte_count, transcendentals=0),
        compiler_params=pltpu.CompilerParams(vmem_limit_bytes=None if far else 24 * 2**20),
    )(*inputs)


def shape(rows, dtype):
    return jax.ShapeDtypeStruct((rows, BLOCK), dtype)


def paired(piece):
    return lax.all_gather(piece, "unit", axis=0, tiled=True, axis_index_groups=[[0, 1], [2, 3], [4, 5], [6, 7]])


PAIRS = [(u, u ^ 1) for u in range(8)]


def neighbours(piece):
    found = []
    for m in (2, 6, 4):
        found.append(lax.ppermute(piece, "unit", [(u, u ^ m) for u in range(8)]))
    return found


def exchange(piece):
    near, second, far = neighbours(piece)
    near, pair = lax.optimization_barrier((near, paired(piece)))
    pieces = [piece, pair]
    for x in (near, far, second):
        pieces += [x, lax.ppermute(x, "unit", PAIRS)]
    return pieces


def shards(
    initial_rates,
    prior_rates,
    local_weight,
    long_weight,
    input_weight,
    unit_bias,
    leak_rate,
    stimulus,
    link_source,
    link_block,
    link_delay,
):
    area_here = lax.axis_index("area")
    unit_here = lax.axis_index("unit")
    order = unit_here ^ jnp.arange(8, dtype=jnp.int32)
    place = link_block ^ (unit_here * (ROWS // BLOCK))
    block_row = link_delay * BLOCKS + place
    from_here = link_source == area_here
    send_rows = jnp.sum(jnp.where(from_here, block_row, 0), axis=1)
    own_source = lax.dynamic_index_in_dim(link_source, area_here, 0, keepdims=False)
    core = jnp.full((8,), unit_here % 2, jnp.int32)
    live = jnp.any(from_here, axis=1)
    late = (send_rows >= BLOCKS // 2) & (send_rows < BLOCKS)
    areas = jnp.arange(BLOCKS, dtype=jnp.int32)
    stages = jnp.arange(2, dtype=jnp.int32)
    chosen = live[None, :] & (late.astype(jnp.int32)[None, :] == stages[:, None])
    ahead = chosen[:, None, :] & (areas[None, None, :] < areas[None, :, None])
    place = jnp.sum(ahead.astype(jnp.int32), axis=2)
    here = chosen[:, None, :] & (place[:, None, :] == areas[None, :, None])
    lists = jnp.sum(jnp.where(here, areas[None, None, :], 0), axis=2).astype(jnp.int32)
    counts = jnp.sum(chosen.astype(jnp.int32), axis=1).astype(jnp.int32)
    table = jnp.concatenate([send_rows, own_source, core, order]).astype(jnp.int32)
    tables = [table, lists, counts]
    weight_local = local_weight[0]
    weight_long = long_weight[0]
    inputs = [input_weight[0].T, stimulus, unit_bias, leak_rate]
    drives, leak = call(
        drive_kernel,
        inputs,
        (jax.ShapeDtypeStruct((2 * WINDOWS, ROWS, BLOCK), F32), shape(ROWS, F32)),
        1000,
        [*(pltpu.VMEM(x.shape, x.dtype) for x in inputs[:4]), pltpu.SemaphoreType.DMA((4,))],
        far=4,
    )
    flops = ROWS * UNITS * BLOCK

    def long_range(outgoing):
        arrived = lax.all_to_all(outgoing, "area", split_axis=0, concat_axis=0, tiled=True)
        other = lax.ppermute(arrived, "unit", PAIRS)
        return arrived, other

    gather_scratch = [pltpu.VMEM((16 * BLOCK, BLOCK), BF16)]
    history = shape(UNITS, BF16)
    parcels = jax.ShapeDtypeStruct((BLOCKS, HALF, BLOCK), BF16)
    half_history = shape(UNITS // 2, BF16)
    both = call(
        both_kernel,
        [initial_rates[0], prior_rates[0]],
        shape(2 * ROWS, BF16),
        1000,
        [pltpu.VMEM((ROWS, BLOCK), F32), pltpu.SemaphoreType.DMA((2,))],
        far=2,
    )
    near, second, far = neighbours(both)
    own = paired(both)
    far, drives, leak = lax.optimization_barrier((far, drives, leak))
    near = paired(near)
    pairs = [own, near, far, lax.ppermute(far, "unit", PAIRS), paired(second)]
    *later, outgoing = call(
        start_kernel, [*tables, *pairs], (half_history, half_history, parcels), 1000, [pltpu.VMEM((UNITS, BLOCK), BF16)]
    )

    def window(step, carry):
        later, outgoing, rates = carry
        mine, theirs = long_range(outgoing)
        drive = [drives[2 * step + n] for n in range(2)]
        partial = call(local_kernel, [table, weight_local, *later, drive[0]], shape(ROWS, F32), 2 * flops)
        current, rates, copy = call(
            first_kernel,
            [table, weight_long, mine, theirs, partial, rates, leak],
            (shape(ROWS, F32), shape(ROWS, F32), shape(ROWS, BF16)),
            flops,
            gather_scratch,
        )
        pieces = exchange(copy)
        partial, before = call(
            early_kernel,
            [table, weight_local, *pieces[:4], current, drive[1]],
            (shape(ROWS, F32), shape(4 * ROWS, BF16)),
            flops,
        )
        earlier, rates, copy = call(
            second_kernel,
            [table, weight_local, *pieces[4:], before, partial, rates, leak],
            (history, shape(ROWS, F32), shape(ROWS, BF16)),
            flops,
        )
        pieces = exchange(copy)
        if step == WINDOWS - 1:
            scratch = [pltpu.VMEM((UNITS // 2, BLOCK), BF16)]
            outgoing = call(last_begin_kernel, [*tables, *pieces[:4], earlier], parcels, 1000, scratch)
            inputs = [*tables, *pieces[4:], outgoing]
            return None, call(last_finish_kernel, inputs, parcels, 1000, scratch, {7: 0}), rates
        keep = ((half_history, parcels), 1000)
        front, outgoing = call(begin_kernel, [*tables, *pieces[:4], earlier], *keep)
        back, outgoing = call(finish_kernel, [*tables, *pieces[4:], outgoing], *keep, aliases={7: 1})
        later = [front, back]
        return later, outgoing, rates

    carry = (later, outgoing, initial_rates[0])
    for step in range(WINDOWS):
        carry = window(step, carry)
    later, outgoing, rates = carry
    mine, theirs = long_range(outgoing)
    rates = call(copy_kernel, [rates], shape(ROWS, F32), 1000)
    final_current = call(current_kernel, [table, weight_long, mine, theirs], shape(ROWS, F32), flops, gather_scratch)
    return (rates[None], final_current[None])


def solution(mesh):
    return jax.shard_map(
        shards,
        mesh=mesh,
        in_specs=(
            P("area", "unit", None),
            P("area", "unit", None),
            P("area", "unit", None),
            P("area", "unit", None),
            P("area", "unit", None),
            P("area", "unit"),
            P("area", "unit"),
            P(),
            P(),
            P(),
            P(),
        ),
        out_specs=(P("area", "unit", None), P("area", "unit", None)),
        check_vma=False,
    )
```

```python
import functools

import jax
import jax.numpy as jnp
from jax import lax
from jax.experimental import pallas as pl
from jax.experimental.pallas import tpu as pltpu
from jax.sharding import PartitionSpec as P


UNITS = 4096
BLOCK = 128
WINDOWS = 3
ROWS = 512
HALF = BLOCK // 2
BLOCKS = UNITS // BLOCK


VMEM = pl.BlockSpec(memory_space=pltpu.VMEM)
SMEM = pl.BlockSpec(memory_space=pltpu.SMEM)
HBM = pl.BlockSpec(memory_space=pltpu.HBM)
F32 = jnp.float32
BF16 = jnp.bfloat16

SRC, CORE, UNIT = 32, 48, 56


def put(pieces, first, full):
    for m, piece in enumerate(pieces):
        full[(first + m) * ROWS : (first + m + 1) * ROWS, :] = piece[...]


def put_own(table, piece, pair, full):
    other = pl.multiple_of((1 - table[CORE]) * ROWS, ROWS)
    full[0:ROWS, :] = piece[...]
    full[ROWS : 2 * ROWS, :] = pair[pl.ds(other, ROWS), :]


def by_rows(work):
    def one(i, carry):
        work(pl.ds(pl.multiple_of(i * (ROWS // 2), ROWS // 2), ROWS // 2))
        return carry

    lax.fori_loop(0, 2, one, 0)


def send(table, lists, counts, stage, sources, outgoing):
    half = table[CORE] * HALF

    def one(i, carry):
        area = lists[stage, i]
        row = table[area]
        for array, first in sources:
            count = array.shape[0] // BLOCK

            @pl.when((row >= first) & (row < first + count))
            def _():
                start = pl.multiple_of((row - first) * BLOCK + half, HALF)
                outgoing[area] = array[pl.ds(start, HALF), :]

        return carry

    lax.fori_loop(0, counts[stage], one, 0)


def product(table, weight, rows, full, first):
    total = None
    for m in range(full.shape[0] // ROWS):
        columns = pl.ds(pl.multiple_of(table[UNIT + first + m] * ROWS, ROWS), ROWS)
        part = jnp.dot(weight[rows, columns], full[m * ROWS : (m + 1) * ROWS, :], preferred_element_type=F32)
        total = part if total is None else total + part
    return total


def begin_kernel(table, lists, counts, piece, pair, near, near_other, earlier, front, outgoing):
    put_own(table, piece, pair, front)
    put((near, near_other), 2, front)
    send(table, lists, counts, 0, ((front, 0), (earlier, BLOCKS)), outgoing)


def finish_kernel(table, lists, counts, *refs):
    *pieces, begun, back, outgoing = refs
    del begun
    put(pieces, 0, back)
    send(table, lists, counts, 1, ((back, BLOCKS // 2),), outgoing)


def last_begin_kernel(*refs):
    *inputs, outgoing, front = refs
    begin_kernel(*inputs, front, outgoing)


def last_finish_kernel(*refs):
    *inputs, outgoing, back = refs
    finish_kernel(*inputs, back, outgoing)


def copy_kernel(source, out):
    out[...] = source[...]


def start_kernel(table, lists, counts, own, near, far, far_other, second, front, back, outgoing, earlier):
    mine = pl.multiple_of(table[CORE] * 2 * ROWS, 2 * ROWS)
    theirs = pl.multiple_of(2 * ROWS - mine, 2 * ROWS)
    for m, (piece, row) in enumerate(
        ((own, mine), (own, theirs), (near, mine), (near, theirs), (far, 0), (far_other, 0), (second, mine), (second, theirs))
    ):
        full, first = (front, m * ROWS) if m < 4 else (back, (m - 4) * ROWS)
        full[first : first + ROWS, :] = piece[pl.ds(row, ROWS), :]
        earlier[m * ROWS : (m + 1) * ROWS, :] = piece[pl.ds(row + ROWS, ROWS), :]
    send(table, lists, counts, 0, ((front, 0), (earlier, BLOCKS)), outgoing)
    send(table, lists, counts, 1, ((back, BLOCKS // 2),), outgoing)


def local_kernel(table, weight, front, back, drive, out):
    @by_rows
    def _(rows):
        total = product(table, weight, rows, front, 0) + product(table, weight, rows, back, 4)
        out[rows, :] = drive[rows, :] + total


def collect(table, mine, theirs, inputs):
    half = pl.multiple_of(table[CORE] * HALF, HALF)
    other = pl.multiple_of(HALF - half, HALF)
    for slot in range(16):
        area = table[SRC + slot]
        inputs[pl.ds(slot * BLOCK + half, HALF), :] = mine[area]
        inputs[pl.ds(slot * BLOCK + other, HALF), :] = theirs[area]


def current_kernel(table, weight, mine, theirs, current, inputs):
    collect(table, mine, theirs, inputs)

    @by_rows
    def _(rows):
        current[rows, :] = jnp.dot(weight[rows, :], inputs[...], preferred_element_type=F32)


def moved(rates, leak, drive):
    return rates + leak * (jnp.tanh(drive) - rates)


def first_kernel(table, weight, mine, theirs, partial, rates, leak, current, out, copy, inputs):
    collect(table, mine, theirs, inputs)

    @by_rows
    def _(rows):
        now = jnp.dot(weight[rows, :], inputs[...], preferred_element_type=F32)
        current[rows, :] = now
        new = moved(rates[rows, :], leak[rows, :], partial[rows, :] + now)
        out[rows, :] = new
        copy[rows, :] = new.astype(BF16)


def early_kernel(table, weight, piece, pair, *refs):
    *pieces, current, drive, out, full = refs
    put_own(table, piece, pair, full)
    put(pieces, 2, full)

    @by_rows
    def _(rows):
        total = product(table, weight, rows, full, 0)
        out[rows, :] = current[rows, :] + drive[rows, :] + total


def second_kernel(table, weight, *refs):
    *pieces, before, partial, rates, leak, full, out, copy = refs
    size = before.shape[0]
    full[0:size, :] = before[...]
    put(pieces, size // ROWS, full)

    @by_rows
    def _(rows):
        total = product(table, weight, rows, full.at[pl.ds(size, UNITS - size), :], size // ROWS)
        new = moved(rates[rows, :], leak[rows, :], partial[rows, :] + total)
        out[rows, :] = new
        copy[rows, :] = new.astype(BF16)


def column(row):
    return jnp.transpose(jnp.broadcast_to(row, (BLOCK, row.shape[1])))


def fetch(sources, places, done):
    copies = [pltpu.make_async_copy(x, y, done.at[i]) for i, (x, y) in enumerate(zip(sources, places))]
    for copy in copies:
        copy.start()
    for copy in copies:
        copy.wait()


def drive_kernel(start, *refs):
    out, leak_out, weight, stimulus, bias, leak, done = refs[-7:]
    fetch(refs[:4], (weight, stimulus, bias, leak), done)
    leak_out[...] = column(leak[...])
    base = column(bias[...])

    def one(n, carry):
        part = lax.dot_general(weight[...], stimulus[start + n], (((0,), (0,)), ((), ())), preferred_element_type=F32)
        out[n] = part + base
        return carry

    lax.fori_loop(0, out.shape[0], one, 0)


def both_kernel(rates, prior, out, rates_here, done):
    fetch((rates, prior), (rates_here, out.at[ROWS : 2 * ROWS, :]), done)
    out[0:ROWS, :] = rates_here[...].astype(BF16)


def call(kernel, inputs, outs, flops, scratch=(), aliases=None, far=0):
    byte_count = sum(x.size * x.dtype.itemsize for x in inputs)
    return pl.pallas_call(
        kernel,
        out_shape=outs,
        in_specs=[HBM if i < far else SMEM if x.dtype == jnp.int32 else VMEM for i, x in enumerate(inputs)],
        out_specs=jax.tree.map(lambda _: VMEM, outs),
        scratch_shapes=list(scratch),
        input_output_aliases=aliases or {},
        cost_estimate=pl.CostEstimate(flops=flops, bytes_accessed=byte_count, transcendentals=0),
        compiler_params=pltpu.CompilerParams(vmem_limit_bytes=None if far else 24 * 2**20),
    )(*inputs)


def shape(rows, dtype):
    return jax.ShapeDtypeStruct((rows, BLOCK), dtype)


def paired(piece):
    return lax.all_gather(piece, "unit", axis=0, tiled=True, axis_index_groups=[[0, 1], [2, 3], [4, 5], [6, 7]])


PAIRS = [(u, u ^ 1) for u in range(8)]


def neighbours(piece):
    found = []
    for m in (2, 6, 4):
        found.append(lax.ppermute(piece, "unit", [(u, u ^ m) for u in range(8)]))
    return found


def exchange(piece):
    near, second, far = neighbours(piece)
    near, pair = lax.optimization_barrier((near, paired(piece)))
    pieces = [piece, pair]
    for x in (near, far, second):
        pieces += [x, lax.ppermute(x, "unit", PAIRS)]
    return pieces


def shards(
    initial_rates,
    prior_rates,
    local_weight,
    long_weight,
    input_weight,
    unit_bias,
    leak_rate,
    stimulus,
    link_source,
    link_block,
    link_delay,
):
    area_here = lax.axis_index("area")
    unit_here = lax.axis_index("unit")
    order = unit_here ^ jnp.arange(8, dtype=jnp.int32)
    place = link_block ^ (unit_here * (ROWS // BLOCK))
    block_row = link_delay * BLOCKS + place
    from_here = link_source == area_here
    send_rows = jnp.sum(jnp.where(from_here, block_row, 0), axis=1)
    own_source = lax.dynamic_index_in_dim(link_source, area_here, 0, keepdims=False)
    core = jnp.full((8,), unit_here % 2, jnp.int32)
    live = jnp.any(from_here, axis=1)
    late = (send_rows >= BLOCKS // 2) & (send_rows < BLOCKS)
    areas = jnp.arange(BLOCKS, dtype=jnp.int32)
    stages = jnp.arange(2, dtype=jnp.int32)
    chosen = live[None, :] & (late.astype(jnp.int32)[None, :] == stages[:, None])
    ahead = chosen[:, None, :] & (areas[None, None, :] < areas[None, :, None])
    place = jnp.sum(ahead.astype(jnp.int32), axis=2)
    here = chosen[:, None, :] & (place[:, None, :] == areas[None, :, None])
    lists = jnp.sum(jnp.where(here, areas[None, None, :], 0), axis=2).astype(jnp.int32)
    counts = jnp.sum(chosen.astype(jnp.int32), axis=1).astype(jnp.int32)
    table = jnp.concatenate([send_rows, own_source, core, order]).astype(jnp.int32)
    tables = [table, lists, counts]
    weight_local = local_weight[0]
    weight_long = long_weight[0]
    inputs = [input_weight[0].T, stimulus, unit_bias, leak_rate]

    def driven(start, count):
        return call(
            functools.partial(drive_kernel, start),
            inputs,
            (jax.ShapeDtypeStruct((count, ROWS, BLOCK), F32), shape(ROWS, F32)),
            1000,
            [*(pltpu.VMEM(x.shape, x.dtype) for x in inputs[:4]), pltpu.SemaphoreType.DMA((4,))],
            far=4,
        )

    drives, leak = driven(0, 2)
    late_drives, _ = driven(2, 2 * WINDOWS - 2)
    flops = ROWS * UNITS * BLOCK

    def long_range(outgoing):
        arrived = lax.all_to_all(outgoing, "area", split_axis=0, concat_axis=0, tiled=True)
        other = lax.ppermute(arrived, "unit", PAIRS)
        return arrived, other

    gather_scratch = [pltpu.VMEM((16 * BLOCK, BLOCK), BF16)]
    history = shape(UNITS, BF16)
    parcels = jax.ShapeDtypeStruct((BLOCKS, HALF, BLOCK), BF16)
    half_history = shape(UNITS // 2, BF16)
    both = call(
        both_kernel,
        [initial_rates[0], prior_rates[0]],
        shape(2 * ROWS, BF16),
        1000,
        [pltpu.VMEM((ROWS, BLOCK), F32), pltpu.SemaphoreType.DMA((2,))],
        far=2,
    )
    near, second, far = neighbours(both)
    own = paired(both)
    far, drives, leak = lax.optimization_barrier((far, drives, leak))
    near = paired(near)
    pairs = [own, near, far, lax.ppermute(far, "unit", PAIRS), paired(second)]
    *later, outgoing = call(
        start_kernel, [*tables, *pairs], (half_history, half_history, parcels), 1000, [pltpu.VMEM((UNITS, BLOCK), BF16)]
    )

    def window(step, carry):
        later, outgoing, rates = carry
        mine, theirs = long_range(outgoing)
        drive = [drives[n] if step == 0 else late_drives[2 * step + n - 2] for n in range(2)]
        partial = call(local_kernel, [table, weight_local, *later, drive[0]], shape(ROWS, F32), 2 * flops)
        current, rates, copy = call(
            first_kernel,
            [table, weight_long, mine, theirs, partial, rates, leak],
            (shape(ROWS, F32), shape(ROWS, F32), shape(ROWS, BF16)),
            flops,
            gather_scratch,
        )
        pieces = exchange(copy)
        partial, before = call(
            early_kernel,
            [table, weight_local, *pieces[:4], current, drive[1]],
            (shape(ROWS, F32), shape(4 * ROWS, BF16)),
            flops,
        )
        earlier, rates, copy = call(
            second_kernel,
            [table, weight_local, *pieces[4:], before, partial, rates, leak],
            (history, shape(ROWS, F32), shape(ROWS, BF16)),
            flops,
        )
        pieces = exchange(copy)
        if step == WINDOWS - 1:
            scratch = [pltpu.VMEM((UNITS // 2, BLOCK), BF16)]
            outgoing = call(last_begin_kernel, [*tables, *pieces[:4], earlier], parcels, 1000, scratch)
            inputs = [*tables, *pieces[4:], outgoing]
            return None, call(last_finish_kernel, inputs, parcels, 1000, scratch, {7: 0}), rates
        keep = ((half_history, parcels), 1000)
        front, outgoing = call(begin_kernel, [*tables, *pieces[:4], earlier], *keep)
        back, outgoing = call(finish_kernel, [*tables, *pieces[4:], outgoing], *keep, aliases={7: 1})
        later = [front, back]
        return later, outgoing, rates

    carry = (later, outgoing, initial_rates[0])
    for step in range(WINDOWS):
        carry = window(step, carry)
    later, outgoing, rates = carry
    mine, theirs = long_range(outgoing)
    rates = call(copy_kernel, [rates], shape(ROWS, F32), 1000)
    final_current = call(current_kernel, [table, weight_long, mine, theirs], shape(ROWS, F32), flops, gather_scratch)
    return (rates[None], final_current[None])


def solution(mesh):
    return jax.shard_map(
        shards,
        mesh=mesh,
        in_specs=(
            P("area", "unit", None),
            P("area", "unit", None),
            P("area", "unit", None),
            P("area", "unit", None),
            P("area", "unit", None),
            P("area", "unit"),
            P("area", "unit"),
            P(),
            P(),
            P(),
            P(),
        ),
        out_specs=(P("area", "unit", None), P("area", "unit", None)),
        check_vma=False,
    )
```
